32 devices in a mesh: shard: 8 (over y, x, core), ctx: 4 (over z).
Axes of the slice: x: 2, y: 2, z: 4, core: 2. Of those that a mesh axis runs over, the one named last changes fastest.
Arguments:
- hidden_in: float32 [8, 1024, 1024], P('shard', 'ctx'), may hold values from -6 to 6
- mixer_gain: float32 [1024], replicated, may hold values from 0.5 to 1.5
- mixer_proj: bfloat16 [1024, 3072], P(('shard', 'ctx')), may hold values from -0.1875 to 0.1875
- decay_proj: bfloat16 [1024, 8], P(('shard', 'ctx')), may hold values from -0.1875 to 0.1875
- conv_kernel: float32 [4, 2048], replicated, may hold values from -3 to 3
- decay_log: float32 [4], replicated, may hold values from -1 to 1
- decay_bias: float32 [4], replicated, may hold values from -7 to -2
- output_gain: float32 [256], replicated, may hold values from 0.5 to 1.5
- mixer_out: bfloat16 [1024, 1024], P(('shard', 'ctx')), may hold values from -0.375 to 0.375
- ffn_gain: float32 [1024], replicated, may hold values from 0.5 to 1.5
- ffn_up: bfloat16 [2, 2816, 1024], P(None, ('shard', 'ctx')), may hold values from -0.1875 to 0.1875
- ffn_down: bfloat16 [2816, 1024], P(('shard', 'ctx')), may hold values from -0.109375 to 0.109375
- cotangent: float32 [8, 1024, 1024], P('shard', 'ctx'), may hold values from -6 to 6
Outputs:
- block_out: float32 [8, 1024, 1024], P('shard', 'ctx')
- input_grad: float32 [8, 1024, 1024], P('shard', 'ctx')
- mixer_gain_grad: float32 [1024], replicated
- mixer_proj_grad: float32 [1024, 3072], P(('shard', 'ctx'))
- decay_proj_grad: float32 [1024, 8], P(('shard', 'ctx'))
- conv_kernel_grad: float32 [4, 2048], replicated
- decay_log_grad: float32 [4], replicated
- decay_bias_grad: float32 [4], replicated
- output_gain_grad: float32 [256], replicated
- mixer_out_grad: float32 [1024, 1024], P(('shard', 'ctx'))
- ffn_gain_grad: float32 [1024], replicated
- ffn_up_grad: float32 [2, 2816, 1024], P(None, ('shard', 'ctx'))
- ffn_down_grad: float32 [2816, 1024], P(('shard', 'ctx'))
The draws below stay inside these ranges and needn't reach their ends.
All inputs are finite; a program needn't handle non-finite values.
Results may differ from the reference program's by a relative error of at most 0.025.
The reference program's roundings to bfloat16 on the way (of `normed`, `gated_out`, `ffn_rows`, `activ`, `cot_rows`, `d_one` and `d_proj`) count: a program that leaves them out, or rounds other values in their place, can miss the bound.
Values may be sent and summed in bfloat16 or wider, within the bound.
A program may use at most 192 MiB of HBM per device.

```python
import jax
import jax.numpy as jnp
from jax import lax

D = 1024
H = 4
DK = 128
DV = 256
FF = 2816
CONV = 4
BLOCK = 64
LEN = 1024
QK = 512
VV = 1024
SEQS = 8


def steps_of(key, extent, shards, least, largest):
    def one(dim, parts):
        draws = jax.random.uniform(jax.random.fold_in(jax.random.fold_in(key, 6), dim), (parts,), jnp.float32, least / len(shards), largest / len(shards))
        return jnp.repeat(jnp.exp(draws), extent[dim] // parts).reshape((-1,) + (1,) * (len(extent) - dim - 1))

    level = one(*shards[0])
    for cut in shards[1:]:
        level = level * one(*cut)
    return level


def normal_values(own_key, extent, scale, limit, cuts=(), kind=jnp.bfloat16):
    drawn = jax.random.normal(own_key, extent, jnp.float32) * scale
    if len(cuts) > 0:
        drawn = steps_of(own_key, extent, cuts, -0.22, 0.18) * drawn
    return jnp.clip(drawn, min=-limit, max=limit).astype(kind)


def setup_inputs(seed: int = 0) -> dict:
    keys = jax.random.split(jax.random.key(seed), 14)
    return {
        "hidden_in": normal_values(keys[0], (SEQS, LEN, D), 1.0, 6.0, ((0, 8), (1, 4)), jnp.float32),
        "mixer_gain": jnp.clip(1.0 + 0.1 * jax.random.normal(keys[1], (D,), jnp.float32), 0.5, 1.5),
        "mixer_proj": normal_values(keys[2], (D, 2 * QK + 2 * VV), D ** -0.5, 0.1875, ((0, 32),)),
        "decay_proj": normal_values(keys[3], (D, 2 * H), D ** -0.5, 0.1875, ((0, 32),)),
        "conv_kernel": normal_values(keys[4], (CONV, 2 * QK + VV), 0.5, 3.0, (), jnp.float32),
        "decay_log": jnp.clip(jax.random.uniform(keys[5], (H,), jnp.float32, -1.0, 1.0), -1.0, 1.0),
        "decay_bias": jnp.clip(jax.random.uniform(keys[6], (H,), jnp.float32, -7.0, -2.0), -7.0, -2.0),
        "output_gain": jnp.clip(1.0 + 0.1 * jax.random.normal(keys[7], (DV,), jnp.float32), 0.5, 1.5),
        "mixer_out": normal_values(keys[8], (VV, D), (VV // 4) ** -0.5, 0.375, ((0, 32),)),
        "ffn_gain": jnp.clip(1.0 + 0.1 * jax.random.normal(keys[9], (D,), jnp.float32), 0.5, 1.5),
        "ffn_up": normal_values(keys[10], (2, FF, D), D ** -0.5, 0.1875, ((1, 32),)),
        "ffn_down": normal_values(keys[11], (FF, D), FF ** -0.5, 0.109375, ((0, 32),)),
        "cotangent": normal_values(keys[12], (SEQS, LEN, D), 1.0, 6.0, ((0, 8), (1, 4)), jnp.float32),
    }


norm_eps = 1e-06
exact_mode = lax.Precision.HIGHEST

def block_step(carry_state, queries, keys_in, values_in, decays, beta_in):
    size = decays.shape[-1]
    cumul = jnp.cumsum(decays, axis=-1)
    later = jnp.arange(size)[:, None]
    earlier = jnp.arange(size)[None, :]
    strict = earlier < later
    inclusive = earlier <= later
    spread = cumul[..., :, None] - cumul[..., None, :]
    decay_strict = jnp.where(strict, jnp.exp(jnp.where(strict, spread, 0.0)), 0.0)
    decay_incl = jnp.where(inclusive, jnp.exp(jnp.where(inclusive, spread, 0.0)), 0.0)
    key_key = jnp.einsum('bhtk,bhsk->bhts', keys_in, keys_in, precision=exact_mode)
    query_key = jnp.einsum('bhtk,bhsk->bhts', queries, keys_in, precision=exact_mode)
    lower_mat = jnp.eye(size, dtype=jnp.float32) + beta_in[..., :, None] * decay_strict * key_key
    growth = jnp.exp(cumul)
    seen = jnp.einsum('bhtk,bhkw->bhtw', keys_in, carry_state, precision=exact_mode)
    right_side = beta_in[..., None] * (values_in - growth[..., None] * seen)
    deltas = jax.scipy.linalg.solve_triangular(lower_mat, right_side, lower=True)
    from_state = jnp.einsum('bhtk,bhkw->bhtw', queries, carry_state, precision=exact_mode)
    outputs = growth[..., None] * from_state + jnp.einsum('bhts,bhsw->bhtw', query_key * decay_incl, deltas, precision=exact_mode)
    tail_decay = jnp.exp(cumul[..., -1:] - cumul)
    new_state = jnp.exp(cumul[..., -1])[..., None, None] * carry_state + jnp.einsum('bhsk,bhsw->bhkw', keys_in * tail_decay[..., None], deltas, precision=exact_mode)
    return (new_state, outputs)

def to_blocks(array):
    seq_count, length = (array.shape[0], array.shape[1])
    shaped = array.reshape((seq_count, length // BLOCK, BLOCK) + array.shape[2:])
    if shaped.ndim == 5:
        return shaped.transpose(1, 0, 3, 2, 4)
    return shaped.transpose(1, 0, 3, 2)

def run_blocks(start_state, queries, keys_in, values_in, decays, beta_in):
    seq_count, length = (decays.shape[0], decays.shape[1])

    def advance(carry_state, item):
        return block_step(carry_state, item[0], item[1], item[2], item[3], item[4])
    final_state, outputs = lax.scan(advance, start_state, (to_blocks(queries), to_blocks(keys_in), to_blocks(values_in), to_blocks(decays), to_blocks(beta_in)))
    outputs = outputs.transpose(1, 0, 3, 2, 4).reshape(seq_count, length, H, outputs.shape[-1])
    return (final_state, outputs)

def conv_silu(padded, kernel):
    length = padded.shape[1] - (CONV - 1)
    total = kernel[0] * padded[:, 0:length]
    for offset in range(1, CONV):
        total = total + kernel[offset] * padded[:, offset:offset + length]
    return jax.nn.silu(total)

def split_heads(act, rate_in, decay_log, decay_bias):
    seq_count, length = (act.shape[0], act.shape[1])
    query_raw = act[..., :QK].reshape(seq_count, length, H, DK)
    key_raw = act[..., QK:2 * QK].reshape(seq_count, length, H, DK)
    values_in = act[..., 2 * QK:].reshape(seq_count, length, H, DV)
    queries = query_raw * lax.rsqrt(lax.optimization_barrier(jnp.sum(query_raw * query_raw, -1, keepdims=True)) + norm_eps) * DK ** (-0.5)
    keys_in = key_raw * lax.rsqrt(lax.optimization_barrier(jnp.sum(key_raw * key_raw, -1, keepdims=True)) + norm_eps)
    decays = -jnp.exp(decay_log) * jax.nn.softplus(rate_in[..., :H] + decay_bias)
    beta_in = jax.nn.sigmoid(rate_in[..., H:])
    return (queries, keys_in, values_in, decays, beta_in)

def gate_norm(mixed_out, gate_pre, output_gain):
    seq_count, length = (gate_pre.shape[0], gate_pre.shape[1])
    gate_heads = gate_pre.reshape(seq_count, length, H, DV)
    scaled = mixed_out * lax.rsqrt(lax.optimization_barrier(jnp.mean(mixed_out * mixed_out, -1, keepdims=True)) + norm_eps)
    return (scaled * output_gain * jax.nn.silu(gate_heads)).reshape(seq_count, length, H * DV)

def mixer_core(padded, rate_in, gate_pre, kernel, decay_log, decay_bias, output_gain):
    act = conv_silu(padded, kernel)
    queries, keys_in, values_in, decays, beta_in = split_heads(act, rate_in, decay_log, decay_bias)
    start_state = jnp.zeros((decays.shape[0], H, DK, DV), jnp.float32)
    final_state, mixed_out = run_blocks(start_state, queries, keys_in, values_in, decays, beta_in)
    return gate_norm(mixed_out, gate_pre, output_gain)

def rms_back(inputs, scale, gain, upstream):
    unit = inputs * scale
    weighted = upstream * gain
    gain_grad = lax.optimization_barrier(jnp.sum(upstream * unit, axis=0))
    return (scale * (weighted - unit * lax.optimization_barrier(jnp.mean(weighted * unit, -1, keepdims=True))), gain_grad)

def ffn_local(ffn_rows, cot_rows, up_weight, down_weight):
    up_one = jnp.dot(ffn_rows.astype(jnp.float32), up_weight[0].T.astype(jnp.float32), preferred_element_type=jnp.float32)
    up_two = jnp.dot(ffn_rows.astype(jnp.float32), up_weight[1].T.astype(jnp.float32), preferred_element_type=jnp.float32)
    sigma = jax.nn.sigmoid(up_one)
    activ = (up_one * sigma * up_two).astype(jnp.bfloat16)
    ffn_part = jnp.dot(activ.astype(jnp.float32), down_weight.astype(jnp.float32), preferred_element_type=jnp.float32)
    d_activ = jnp.dot(cot_rows.astype(jnp.float32), down_weight.T.astype(jnp.float32), preferred_element_type=jnp.float32)
    d_one = (d_activ * up_two * sigma * (1.0 + up_one * (1.0 - sigma))).astype(jnp.bfloat16)
    d_two = (d_activ * up_one * sigma).astype(jnp.bfloat16)
    down_grad = jnp.dot(activ.T.astype(jnp.float32), cot_rows.astype(jnp.float32), preferred_element_type=jnp.float32)
    up_grad = jnp.stack([jnp.dot(d_one.T.astype(jnp.float32), ffn_rows.astype(jnp.float32), preferred_element_type=jnp.float32), jnp.dot(d_two.T.astype(jnp.float32), ffn_rows.astype(jnp.float32), preferred_element_type=jnp.float32)])
    d_input = jnp.dot(d_one.astype(jnp.float32), up_weight[0].astype(jnp.float32), preferred_element_type=jnp.float32) + jnp.dot(d_two.astype(jnp.float32), up_weight[1].astype(jnp.float32), preferred_element_type=jnp.float32)
    return (ffn_part, d_input, up_grad, down_grad)

def reference(hidden_in, mixer_gain, mixer_proj, decay_proj, conv_kernel, decay_log, decay_bias, output_gain, mixer_out, ffn_gain, ffn_up, ffn_down, cotangent):
    conv_width = 2 * QK + VV

    def one_sequence(totals, item):
        flat_in, cot_flat = item
        scale_in = lax.rsqrt(lax.optimization_barrier(jnp.mean(flat_in * flat_in, -1, keepdims=True)) + norm_eps)
        normed = (flat_in * scale_in * mixer_gain).astype(jnp.bfloat16)
        projected = jnp.dot(normed.astype(jnp.float32), mixer_proj.astype(jnp.float32), preferred_element_type=jnp.float32)
        pre_rows = projected[:, :conv_width]
        gate_pre = projected[:, conv_width:]
        rate_in = jnp.dot(normed.astype(jnp.float32), decay_proj.astype(jnp.float32), preferred_element_type=jnp.float32)
        padded = jnp.concatenate([jnp.zeros((CONV - 1, conv_width), jnp.float32), pre_rows], 0)[None]
        gated_out, core_back = jax.vjp(mixer_core, padded, rate_in[None], gate_pre[None], conv_kernel, decay_log, decay_bias, output_gain)
        gated_rows = gated_out[0].astype(jnp.bfloat16)
        residual = flat_in + jnp.dot(gated_rows.astype(jnp.float32), mixer_out.astype(jnp.float32), preferred_element_type=jnp.float32)
        scale_mid = lax.rsqrt(lax.optimization_barrier(jnp.mean(residual * residual, -1, keepdims=True)) + norm_eps)
        ffn_rows = (residual * scale_mid * ffn_gain).astype(jnp.bfloat16)
        cot_rows = cot_flat.astype(jnp.bfloat16)
        ffn_sum, d_ffn, up_grad, down_grad = ffn_local(ffn_rows, cot_rows, ffn_up, ffn_down)
        block_out = residual + ffn_sum
        d_res_part, gain_two_grad = rms_back(residual, scale_mid, ffn_gain, d_ffn)
        d_residual = cot_flat + d_res_part
        d_res_rows = d_residual.astype(jnp.bfloat16)
        out_grad = jnp.dot(gated_rows.T.astype(jnp.float32), d_res_rows.astype(jnp.float32), preferred_element_type=jnp.float32)
        d_gated = jnp.dot(d_res_rows.astype(jnp.float32), mixer_out.T.astype(jnp.float32), preferred_element_type=jnp.float32)
        d_padded, d_rate, d_gate, kernel_grad, log_grad, bias_grad, gain_out_grad = core_back(d_gated[None])
        d_proj = jnp.concatenate([d_padded[0, CONV - 1:], d_gate[0]], 1).astype(jnp.bfloat16)
        d_rate_rows = d_rate[0].astype(jnp.bfloat16)
        proj_grad = jnp.dot(normed.T.astype(jnp.float32), d_proj.astype(jnp.float32), preferred_element_type=jnp.float32)
        rate_grad = jnp.dot(normed.T.astype(jnp.float32), d_rate_rows.astype(jnp.float32), preferred_element_type=jnp.float32)
        d_normed = jnp.dot(d_proj.astype(jnp.float32), mixer_proj.T.astype(jnp.float32), preferred_element_type=jnp.float32) + jnp.dot(d_rate_rows.astype(jnp.float32), decay_proj.T.astype(jnp.float32), preferred_element_type=jnp.float32)
        d_in_part, gain_one_grad = rms_back(flat_in, scale_in, mixer_gain, d_normed)
        input_grad = d_residual + d_in_part
        grads = (gain_one_grad, proj_grad, rate_grad, kernel_grad, log_grad, bias_grad, gain_out_grad, out_grad, gain_two_grad, up_grad, down_grad)
        return (jax.tree.map(lambda left, right: left + right, totals, grads), (block_out, input_grad))
    start = (jnp.zeros((D,), jnp.float32), jnp.zeros((D, 2 * QK + 2 * VV), jnp.float32), jnp.zeros((D, 2 * H), jnp.float32), jnp.zeros((CONV, conv_width), jnp.float32), jnp.zeros((H,), jnp.float32), jnp.zeros((H,), jnp.float32), jnp.zeros((DV,), jnp.float32), jnp.zeros((VV, D), jnp.float32), jnp.zeros((D,), jnp.float32), jnp.zeros((2, FF, D), jnp.float32), jnp.zeros((FF, D), jnp.float32))
    totals, (block_out, input_grad) = lax.scan(one_sequence, start, (hidden_in, cotangent))
    return (block_out, input_grad, totals[0], totals[1], totals[2], totals[3], totals[4], totals[5], totals[6], totals[7], totals[8], totals[9], totals[10])
```

```python
import functools

import jax
import jax.numpy as jnp
from jax import lax
from jax.experimental import pallas as pl
from jax.experimental.pallas import tpu as pltpu
from jax.sharding import PartitionSpec as P

H = 4
DK = 128
DV = 256
CONV = 4
QK = 512
VV = 1024
LANE = 128

norm_eps = 1e-06
exact_mode = lax.Precision.HIGHEST
F32 = jnp.float32
BF16 = jnp.bfloat16
ALL = ("shard", "ctx")


def dot(a, b, ca=1, cb=0):
    return lax.dot_general(
        a, b, (((ca,), (cb,)), ((), ())), precision=exact_mode, preferred_element_type=F32
    )


def low(a, b, ca=1, cb=0):
    return lax.dot_general(
        a.astype(BF16), b.astype(BF16), (((ca,), (cb,)), ((), ())), preferred_element_type=F32
    )


def column(ref, h):
    x = ref[...]
    lanes = lax.broadcasted_iota(jnp.int32, x.shape, 1)
    return jnp.sum(jnp.where(lanes == h, x, 0.0), 1, keepdims=True)


def unit(raw):
    r = lax.rsqrt(jnp.sum(raw * raw, -1, keepdims=True) + norm_eps)
    return raw * r, r


def iotas(size):
    return (
        lax.broadcasted_iota(jnp.int32, (size, size), 0),
        lax.broadcasted_iota(jnp.int32, (size, size), 1),
    )


def unit_lower_inverse(a):
    size = a.shape[0]
    row, col = iotas(size)
    apart = jnp.bitwise_xor(row, col)
    x = jnp.where(row == col, 1.0, 0.0) - jnp.where(apart == 1, a, 0.0)
    b = 2
    while b < size:
        c = jnp.where((apart >= b) & (apart < 2 * b), a, 0.0)
        x = x - dot(dot(x, c), x)
        b *= 2
    return x


def pair_terms(q, k, gc, gr, beta):
    row, col = iotas(k.shape[0])
    incl = col <= row
    decay = jnp.where(incl, jnp.exp(jnp.where(incl, gc - gr, 0.0)), 0.0)
    kk = dot(k, k, 1, 1)
    qk = dot(q, k, 1, 1)
    below = jnp.where(col < row, decay * kk, 0.0)
    return decay, below, qk * decay, row, col


def core_fwd(q_ref, k_ref, v_ref, g_ref, gr_ref, b_ref, out_ref, map_ref, state_ref, t_ref):
    h = pl.program_id(1)
    q = unit(q_ref[...])[0] * DK ** (-0.5)
    k = unit(k_ref[...])[0]
    gc, gr, beta = column(g_ref, h), gr_ref[...], column(b_ref, h)
    decay, below, p, row, col = pair_terms(q, k, gc, gr, beta)
    t = unit_lower_inverse(beta * below)
    t_ref[...] = t
    growth = jnp.exp(gc)
    size = k.shape[0]
    right = jnp.concatenate([beta * v_ref[...], (beta * growth) * k], 1)
    solved = dot(t, right)
    mixed = dot(p, solved)
    out_ref[...] = mixed[:, :DV]
    map_ref[...] = growth * q - mixed[:, DV:]
    last = gc[size - 1 : size, :]
    state = dot(k * jnp.exp(last - gc), solved, 0, 0)
    r, c = iotas(DK)
    state_ref[:, :DV] = state[:, :DV].astype(BF16)
    state_ref[:, DV:] = (jnp.where(r == c, jnp.exp(last), 0.0) - state[:, DV:]).astype(BF16)


def gate_fwd(place_ref, all_ref, out_ref, map_ref, gate_ref, gain_ref, gated_ref, s0_ref):
    place = place_ref[0]
    devices = all_ref.shape[0]
    s = jnp.zeros((DK, DV), F32)
    for j in range(devices - 1):
        entry = all_ref[j].astype(F32)
        s = jnp.where(j < place, dot(entry[:, DV:], s) + entry[:, :DV], s)
    s0_ref[...] = s
    m = out_ref[...] + dot(map_ref[...], s)
    u = m * lax.rsqrt(jnp.mean(m * m, -1, keepdims=True) + norm_eps)
    g = gate_ref[...]
    gated_ref[...] = (u * gain_ref[...] * (g * jax.nn.sigmoid(g))).astype(BF16)


def gate_bwd(dy_ref, out_ref, map_ref, s0_ref, gate_ref, gain_ref, dm_ref, dg_ref, ds_ref, dgain_ref):
    m = out_ref[...] + dot(map_ref[...], s0_ref[...])
    r = lax.rsqrt(jnp.mean(m * m, -1, keepdims=True) + norm_eps)
    u = m * r
    g, gain, dy = gate_ref[...], gain_ref[...], dy_ref[...]
    sg = jax.nn.sigmoid(g)
    silu = g * sg
    dg_ref[...] = (dy * u * gain * (sg * (1.0 + g * (1.0 - sg)))).astype(BF16)
    dgain_ref[...] = jnp.sum(dy * u * silu, 0, keepdims=True)
    du = dy * gain * silu
    dm = r * (du - u * jnp.mean(du * u, -1, keepdims=True))
    dm_ref[...] = dm
    ds_ref[...] = dot(map_ref[...], dm, 0, 0).astype(BF16)


def core_bwd(
    place_ref, maps_ref, ds_all_ref, q_ref, k_ref, v_ref, g_ref, gr_ref, b_ref, t_ref, s0_ref,
    do_ref, dq_ref, dk_ref, dv_ref, dcol_ref, drow_ref,
):
    h = pl.program_id(1)
    place = place_ref[0]
    devices = maps_ref.shape[0]
    ds = jnp.zeros((DK, DV), F32)
    for j in range(devices - 1, 0, -1):
        new = dot(maps_ref[j].astype(F32), ds, 0, 0) + ds_all_ref[j].astype(F32)
        ds = jnp.where(j > place, new, ds)
    qu, rq = unit(q_ref[...])
    q = qu * DK ** (-0.5)
    k, rk = unit(k_ref[...])
    gc, gr, beta = column(g_ref, h), gr_ref[...], column(b_ref, h)
    decay, below, p, row, col = pair_terms(q, k, gc, gr, beta)
    t, s0, do = t_ref[...], s0_ref[...], do_ref[...]
    growth = jnp.exp(gc)
    size = k.shape[0]
    last = gc[size - 1 : size, :]
    tail = jnp.exp(last - gc)
    kd = k * tail
    seen = dot(k, s0)
    rest = v_ref[...] - growth * seen
    x = dot(t, beta * rest)
    qs = dot(q, s0)
    dx = dot(p, do, 0, 0) + dot(kd, ds)
    dr = dot(t, dx, 0, 0)
    da = jnp.where(col < row, -dot(dr, x, 1, 1), 0.0)
    dp = jnp.where(col <= row, dot(do, x, 1, 1), 0.0)
    dkd = dot(x, ds, 1, 1)
    dv_ref[...] = beta * dr
    dbeta = jnp.sum(dr * rest, 1, keepdims=True) + jnp.sum(da * below, 1, keepdims=True)
    dgrow = jnp.sum(do * qs, 1, keepdims=True) - jnp.sum(beta * dr * seen, 1, keepdims=True)
    dqk = dp * decay
    dkk = da * beta * decay
    dq = dot(growth * do, s0, 1, 1) + dot(dqk, k)
    dk = (
        dot((-beta * growth) * dr, s0, 1, 1)
        + dot(dqk, q, 0, 0)
        + dot(dkk, k)
        + dot(dkk, k, 0, 0)
        + dkd * tail
    )
    dspread = dp * p + da * (beta * below)
    dtail = jnp.sum(dkd * k, 1, keepdims=True) * tail
    dlast = jnp.sum(dtail, 0, keepdims=True) + jnp.exp(last) * jnp.sum(
        jnp.sum(ds * s0, 1, keepdims=True), 0, keepdims=True
    )
    at = lax.broadcasted_iota(jnp.int32, gc.shape, 0)
    dgc = jnp.sum(dspread, 1, keepdims=True) - dtail + dgrow * growth
    dgc = dgc + jnp.where(at == size - 1, dlast, 0.0)
    drow_ref[...] = -jnp.sum(dspread, 0, keepdims=True)
    lane = lax.broadcasted_iota(jnp.int32, dcol_ref.shape, 1)
    dcol_ref[...] = jnp.where(lane == 0, dgc, dbeta)
    du = dq * DK ** (-0.5)
    dq_ref[...] = rq * (du - qu * jnp.sum(du * qu, -1, keepdims=True))
    dk_ref[...] = rk * (dk - k * jnp.sum(dk * k, -1, keepdims=True))


def spec(block, index):
    return pl.BlockSpec(block, index)


def cols(length, width, first=0):
    return spec((None, length, width), lambda b, h: (b, 0, first + h))


def per_head(*block):
    return spec((None, None) + block, lambda b, h: (b, h) + (0,) * len(block))


def gathered(devices, rows, width, at=0):
    return spec((devices, None, None, rows, width), lambda b, h: (0, b, h, 0, at))


def whole(*block):
    return spec((None,) + block, lambda b, h: (b,) + (0,) * len(block))


def call(body, name, seqs, args, in_specs, out_specs, outs, flops):
    size = sum(a.size * a.dtype.itemsize for a in args) + sum(
        o.size * o.dtype.itemsize for o in outs
    )
    return pl.pallas_call(
        body,
        grid=(seqs, H),
        in_specs=in_specs,
        out_specs=out_specs,
        out_shape=outs,
        name=name,
        cost_estimate=pl.CostEstimate(flops=flops, bytes_accessed=size, transcendentals=0),
    )(*args)


def conv_silu(padded, kernel):
    length = padded.shape[1] - (CONV - 1)
    total = kernel[0] * padded[:, 0:length]
    for offset in range(1, CONV):
        total = total + kernel[offset] * padded[:, offset : offset + length]
    return jax.nn.silu(total)


def rates(rate_in, decay_log, decay_bias):
    length = rate_in.shape[1]
    decays = -jnp.exp(decay_log) * jax.nn.softplus(rate_in[..., :H] + decay_bias)
    lower = jnp.tril(jnp.ones((length, length), F32))
    cumul = jnp.einsum("ts,bsh->bth", lower, decays, precision=exact_mode)
    return cumul, jax.nn.sigmoid(rate_in[..., H:])


def shifted(shard, axis, by):
    devices = lax.axis_size(axis)
    pairs = [(i, i + by) for i in range(devices) if 0 <= i + by < devices]
    return lax.ppermute(shard, axis, pairs)


def rms_back(inputs, scale, gain, upstream):
    normal = inputs * scale
    weighted = upstream * gain
    gain_grad = jnp.sum(upstream * normal, axis=0)
    return (scale * (weighted - normal * jnp.mean(weighted * normal, -1, keepdims=True)), gain_grad)


def gather(w):
    return lax.all_gather(w, ALL, axis=0, tiled=True)


def scatter(g):
    return lax.psum_scatter(g.astype(BF16), ALL, scatter_dimension=0, tiled=True).astype(F32)


def mm(a, b):
    return jnp.dot(a, b, preferred_element_type=F32)


def local(
    hidden_in, mixer_gain, mixer_proj, decay_proj, conv_kernel, decay_log, decay_bias,
    output_gain, mixer_out, ffn_gain, ffn_up, ffn_down, cotangent,
):
    seqs, length, feat = hidden_in.shape
    rows = seqs * length
    conv_width = 2 * QK + VV
    proj_cols = conv_width + VV
    rate_cols = 2 * H
    devices = lax.axis_size("ctx")
    place = jnp.reshape(lax.axis_index("ctx"), (1,)).astype(jnp.int32)
    sds = jax.ShapeDtypeStruct

    w_in = gather(
        jnp.concatenate(
            [mixer_proj, decay_proj, jnp.zeros((mixer_proj.shape[0], LANE - rate_cols), BF16)], 1
        )
    )
    w_out = gather(mixer_out)
    up_1, up_2, down = gather(ffn_up[0]), gather(ffn_up[1]), gather(ffn_down)

    flat_in = hidden_in.reshape(rows, feat)
    scale_in = lax.rsqrt(jnp.mean(flat_in * flat_in, -1, keepdims=True) + norm_eps)
    normed = (flat_in * scale_in * mixer_gain).astype(BF16)
    cot_flat = cotangent.reshape(rows, feat)
    cot_rows = cot_flat.astype(BF16)

    projected = mm(normed, w_in).reshape(seqs, length, -1)
    pre_rows = projected[..., :conv_width]
    rate_in = projected[..., proj_cols : proj_cols + rate_cols]
    edge_rows = shifted(pre_rows[:, length - (CONV - 1) :], "ctx", 1)
    padded = jnp.concatenate([edge_rows, pre_rows], 1)
    act, conv_back = jax.vjp(conv_silu, padded, conv_kernel)
    (cumul, beta), rates_back = jax.vjp(rates, rate_in, decay_log, decay_bias)
    cumul_row = jnp.swapaxes(cumul, 1, 2)[:, :, None, :]

    qkv = [cols(length, DK), cols(length, DK, QK // DK), cols(length, DV, 2 * QK // DV)]
    narrow = [whole(length, H), per_head(1, length), whole(length, H)]
    work = seqs * H * length * length * DV
    local_out, query_map, own_state, inverse = call(
        core_fwd, "core_fwd", seqs,
        (act, act, act, cumul, cumul_row, beta),
        qkv + narrow,
        [cols(length, DV), cols(length, DK), per_head(DK, DV + DK), per_head(length, length)],
        [
            sds((seqs, length, VV), F32),
            sds((seqs, length, QK), F32),
            sds((seqs, H, DK, DV + DK), BF16),
            sds((seqs, H, length, length), F32),
        ],
        200 * work,
    )
    states = lax.all_gather(own_state, "ctx")
    gain_row = output_gain.reshape(1, DV)
    gain_spec = spec((1, DV), lambda b, h: (0, 0))
    place_spec = pl.BlockSpec(memory_space=pltpu.SMEM)
    gate_spec = cols(length, DV, conv_width // DV)
    gated, state_in = call(
        gate_fwd, "gate_fwd", seqs,
        (place, states, local_out, query_map, projected, gain_row),
        [place_spec, gathered(devices, DK, DV + DK), cols(length, DV), cols(length, DK),
         gate_spec, gain_spec],
        [cols(length, DV), per_head(DK, DV)],
        [sds((seqs, length, VV), BF16), sds((seqs, H, DK, DV), F32)],
        20 * work,
    )
    gated_rows = gated.reshape(rows, VV)
    residual = flat_in + mm(gated_rows, w_out)
    scale_mid = lax.rsqrt(jnp.mean(residual * residual, -1, keepdims=True) + norm_eps)
    ffn_rows = (residual * scale_mid * ffn_gain).astype(BF16)

    up_one, up_two = mm(ffn_rows, up_1.T), mm(ffn_rows, up_2.T)
    sigma = jax.nn.sigmoid(up_one)
    activ = (up_one * sigma * up_two).astype(BF16)
    block_out = residual + mm(activ, down)
    d_activ = mm(cot_rows, down.T)
    d_one = (d_activ * up_two * sigma * (1.0 + up_one * (1.0 - sigma))).astype(BF16)
    d_two = (d_activ * up_one * sigma).astype(BF16)
    down_shard = scatter(mm(activ.T, cot_rows))
    up_shard = jnp.stack([scatter(mm(d_one.T, ffn_rows)), scatter(mm(d_two.T, ffn_rows))])
    d_ffn = mm(d_one, up_1) + mm(d_two, up_2)

    d_res_part, gain_two_grad = rms_back(residual, scale_mid, ffn_gain, d_ffn)
    d_residual = cot_flat + d_res_part
    d_res_rows = d_residual.astype(BF16)
    out_shard = scatter(mm(gated_rows.T, d_res_rows))
    d_gated = mm(d_res_rows, w_out.T).reshape(seqs, length, VV)
    d_mixed, d_gate, own_ds, gain_out_part = call(
        gate_bwd, "gate_bwd", seqs,
        (d_gated, local_out, query_map, state_in, projected, gain_row),
        [cols(length, DV), cols(length, DV), cols(length, DK), per_head(DK, DV), gate_spec,
         gain_spec],
        [cols(length, DV), cols(length, DV), per_head(DK, DV), per_head(1, DV)],
        [
            sds((seqs, length, VV), F32),
            sds((seqs, length, VV), BF16),
            sds((seqs, H, DK, DV), BF16),
            sds((seqs, H, 1, DV), F32),
        ],
        20 * work,
    )
    d_states = lax.all_gather(own_ds, "ctx")
    d_q, d_k, d_v, d_cols, d_rows = call(
        core_bwd, "core_bwd", seqs,
        (place, states, d_states, act, act, act, cumul, cumul_row, beta, inverse, state_in, d_mixed),
        [place_spec, gathered(devices, DK, DK, DV // DK), gathered(devices, DK, DV)]
        + qkv + narrow
        + [per_head(length, length), per_head(DK, DV), cols(length, DV)],
        [cols(length, DK), cols(length, DK), cols(length, DV), per_head(length, 2),
         per_head(1, length)],
        [
            sds((seqs, length, QK), F32),
            sds((seqs, length, QK), F32),
            sds((seqs, length, VV), F32),
            sds((seqs, H, length, 2), F32),
            sds((seqs, H, 1, length), F32),
        ],
        120 * work,
    )
    d_padded, kernel_grad = conv_back(jnp.concatenate([d_q, d_k, d_v], -1))
    d_cumul = jnp.swapaxes(d_cols[..., 0] + d_rows[:, :, 0], 1, 2)
    d_beta = jnp.swapaxes(d_cols[..., 1], 1, 2)
    d_rate, log_grad, bias_grad = rates_back((d_cumul, d_beta))
    d_edge = shifted(d_padded[:, : CONV - 1], "ctx", -1)
    d_pre = d_padded[:, CONV - 1 :].at[:, length - (CONV - 1) :].add(d_edge)
    d_proj = jnp.concatenate(
        [
            d_pre.reshape(rows, conv_width).astype(BF16),
            d_gate.reshape(rows, VV),
            d_rate.reshape(rows, rate_cols).astype(BF16),
            jnp.zeros((rows, LANE - rate_cols), BF16),
        ],
        1,
    )
    in_shard = scatter(mm(normed.T, d_proj))
    d_normed = mm(d_proj, w_in.T)
    d_in_part, gain_one_grad = rms_back(flat_in, scale_in, mixer_gain, d_normed)
    input_grad = d_residual + d_in_part

    small = (
        gain_one_grad, gain_two_grad, kernel_grad, log_grad, bias_grad,
        jnp.sum(gain_out_part, (0, 1, 2)),
    )
    flat = jnp.concatenate([s.reshape(-1) for s in small])
    pad = -flat.shape[0] % (8 * LANE)
    total = lax.psum(jnp.pad(flat, (0, pad)).reshape(-1, LANE), ALL).reshape(-1)
    sums, start = [], 0
    for s in small:
        sums.append(total[start : start + s.size].reshape(s.shape))
        start += s.size
    return (
        block_out.reshape(seqs, length, feat),
        input_grad.reshape(seqs, length, feat),
        sums[0],
        in_shard[:, :proj_cols],
        in_shard[:, proj_cols : proj_cols + rate_cols],
        sums[2],
        sums[3],
        sums[4],
        sums[5],
        out_shard,
        sums[1],
        up_shard,
        down_shard,
    )


def solution(mesh):
    split = P(ALL, None)
    block = P("shard", "ctx", None)
    up = P(None, ALL, None)
    return jax.shard_map(
        local,
        mesh=mesh,
        in_specs=(block, P(), split, split, P(), P(), P(), P(), split, P(), up, split, block),
        out_specs=(block, block, P(), split, split, P(), P(), P(), P(), split, P(), up, split),
        check_vma=False,
    )
```

```python
import functools

import jax
import jax.numpy as jnp
from jax import lax
from jax.experimental import pallas as pl
from jax.experimental.pallas import tpu as pltpu
from jax.sharding import PartitionSpec as P

H = 4
DK = 128
DV = 256
CONV = 4
QK = 512
VV = 1024
LANE = 128

norm_eps = 1e-06
exact_mode = lax.Precision.HIGHEST
F32 = jnp.float32
BF16 = jnp.bfloat16
ALL = ("shard", "ctx")


def dot(a, b, ca=1, cb=0):
    return lax.dot_general(
        a, b, (((ca,), (cb,)), ((), ())), precision=exact_mode, preferred_element_type=F32
    )


def low(a, b, ca=1, cb=0):
    return lax.dot_general(
        a.astype(BF16), b.astype(BF16), (((ca,), (cb,)), ((), ())), preferred_element_type=F32
    )


def column(ref, h):
    x = ref[...]
    lanes = lax.broadcasted_iota(jnp.int32, x.shape, 1)
    return jnp.sum(jnp.where(lanes == h, x, 0.0), 1, keepdims=True)


def unit(raw):
    r = lax.rsqrt(jnp.sum(raw * raw, -1, keepdims=True) + norm_eps)
    return raw * r, r


def iotas(size):
    return (
        lax.broadcasted_iota(jnp.int32, (size, size), 0),
        lax.broadcasted_iota(jnp.int32, (size, size), 1),
    )


def unit_lower_inverse(a):
    size = a.shape[0]
    row, col = iotas(size)
    apart = jnp.bitwise_xor(row, col)
    x = jnp.where(row == col, 1.0, 0.0) - jnp.where(apart == 1, a, 0.0)
    b = 2
    while b < size:
        c = jnp.where((apart >= b) & (apart < 2 * b), a, 0.0)
        x = x - dot(dot(x, c), x)
        b *= 2
    return x


def pair_terms(q, k, gc, gr, beta):
    row, col = iotas(k.shape[0])
    incl = col <= row
    decay = jnp.where(incl, jnp.exp(jnp.where(incl, gc - gr, 0.0)), 0.0)
    kk = dot(k, k, 1, 1)
    qk = dot(q, k, 1, 1)
    below = jnp.where(col < row, decay * kk, 0.0)
    return decay, below, qk * decay, row, col


def core_fwd(q_ref, k_ref, v_ref, g_ref, gr_ref, b_ref, out_ref, map_ref, state_ref, t_ref):
    h = pl.program_id(1)
    q = unit(q_ref[...])[0] * DK ** (-0.5)
    k = unit(k_ref[...])[0]
    gc, gr, beta = column(g_ref, h), gr_ref[...], column(b_ref, h)
    decay, below, p, row, col = pair_terms(q, k, gc, gr, beta)
    t = unit_lower_inverse(beta * below)
    t_ref[...] = t
    growth = jnp.exp(gc)
    size = k.shape[0]
    right = jnp.concatenate([beta * v_ref[...], (beta * growth) * k], 1)
    solved = dot(t, right)
    mixed = dot(p, solved)
    out_ref[...] = mixed[:, :DV]
    map_ref[...] = growth * q - mixed[:, DV:]
    last = gc[size - 1 : size, :]
    state = dot(k * jnp.exp(last - gc), solved, 0, 0)
    r, c = iotas(DK)
    state_ref[:, :DV] = state[:, :DV].astype(BF16)
    state_ref[:, DV:] = (jnp.where(r == c, jnp.exp(last), 0.0) - state[:, DV:]).astype(BF16)


def gate_fwd(place_ref, all_ref, out_ref, map_ref, gate_ref, gain_ref, gated_ref, s0_ref):
    place = place_ref[0]
    devices = all_ref.shape[0]
    s = jnp.zeros((DK, DV), F32)
    for j in range(devices - 1):
        entry = all_ref[j].astype(F32)
        s = jnp.where(j < place, dot(entry[:, DV:], s) + entry[:, :DV], s)
    s0_ref[...] = s
    m = out_ref[...] + dot(map_ref[...], s)
    u = m * lax.rsqrt(jnp.mean(m * m, -1, keepdims=True) + norm_eps)
    g = gate_ref[...]
    gated_ref[...] = (u * gain_ref[...] * (g * jax.nn.sigmoid(g))).astype(BF16)


def gate_bwd(dy_ref, out_ref, map_ref, s0_ref, gate_ref, gain_ref, dm_ref, dg_ref, ds_ref, dgain_ref):
    m = out_ref[...] + dot(map_ref[...], s0_ref[...])
    r = lax.rsqrt(jnp.mean(m * m, -1, keepdims=True) + norm_eps)
    u = m * r
    g, gain, dy = gate_ref[...], gain_ref[...], dy_ref[...]
    sg = jax.nn.sigmoid(g)
    silu = g * sg
    dg_ref[...] = (dy * u * gain * (sg * (1.0 + g * (1.0 - sg)))).astype(BF16)
    dgain_ref[...] = jnp.sum(dy * u * silu, 0, keepdims=True)
    du = dy * gain * silu
    dm = r * (du - u * jnp.mean(du * u, -1, keepdims=True))
    dm_ref[...] = dm
    ds_ref[...] = dot(map_ref[...], dm, 0, 0).astype(BF16)


def core_bwd(
    place_ref, maps_ref, ds_all_ref, q_ref, k_ref, v_ref, g_ref, gr_ref, b_ref, t_ref, s0_ref,
    do_ref, dq_ref, dk_ref, dv_ref, dcol_ref, drow_ref,
):
    h = pl.program_id(1)
    place = place_ref[0]
    devices = maps_ref.shape[0]
    ds = jnp.zeros((DK, DV), F32)
    for j in range(devices - 1, 0, -1):
        new = dot(maps_ref[j].astype(F32), ds, 0, 0) + ds_all_ref[j].astype(F32)
        ds = jnp.where(j > place, new, ds)
    qu, rq = unit(q_ref[...])
    q = qu * DK ** (-0.5)
    k, rk = unit(k_ref[...])
    gc, gr, beta = column(g_ref, h), gr_ref[...], column(b_ref, h)
    decay, below, p, row, col = pair_terms(q, k, gc, gr, beta)
    t, s0, do = t_ref[...], s0_ref[...], do_ref[...]
    growth = jnp.exp(gc)
    size = k.shape[0]
    last = gc[size - 1 : size, :]
    tail = jnp.exp(last - gc)
    kd = k * tail
    seen = dot(k, s0)
    rest = v_ref[...] - growth * seen
    x = dot(t, beta * rest)
    qs = dot(q, s0)
    dx = dot(p, do, 0, 0) + dot(kd, ds)
    dr = dot(t, dx, 0, 0)
    da = jnp.where(col < row, -dot(dr, x, 1, 1), 0.0)
    dp = jnp.where(col <= row, dot(do, x, 1, 1), 0.0)
    dkd = dot(x, ds, 1, 1)
    dv_ref[...] = beta * dr
    dbeta = jnp.sum(dr * rest, 1, keepdims=True) + jnp.sum(da * below, 1, keepdims=True)
    dgrow = jnp.sum(do * qs, 1, keepdims=True) - jnp.sum(beta * dr * seen, 1, keepdims=True)
    dqk = dp * decay
    dkk = da * beta * decay
    dq = dot(growth * do, s0, 1, 1) + dot(dqk, k)
    dk = (
        dot((-beta * growth) * dr, s0, 1, 1)
        + dot(dqk, q, 0, 0)
        + dot(dkk, k)
        + dot(dkk, k, 0, 0)
        + dkd * tail
    )
    dspread = dp * p + da * (beta * below)
    dtail = jnp.sum(dkd * k, 1, keepdims=True) * tail
    dlast = jnp.sum(dtail, 0, keepdims=True) + jnp.exp(last) * jnp.sum(
        jnp.sum(ds * s0, 1, keepdims=True), 0, keepdims=True
    )
    at = lax.broadcasted_iota(jnp.int32, gc.shape, 0)
    dgc = jnp.sum(dspread, 1, keepdims=True) - dtail + dgrow * growth
    dgc = dgc + jnp.where(at == size - 1, dlast, 0.0)
    drow_ref[...] = -jnp.sum(dspread, 0, keepdims=True)
    lane = lax.broadcasted_iota(jnp.int32, dcol_ref.shape, 1)
    dcol_ref[...] = jnp.where(lane == 0, dgc, dbeta)
    du = dq * DK ** (-0.5)
    dq_ref[...] = rq * (du - qu * jnp.sum(du * qu, -1, keepdims=True))
    dk_ref[...] = rk * (dk - k * jnp.sum(dk * k, -1, keepdims=True))


def spec(block, index):
    return pl.BlockSpec(block, index)


def cols(length, width, first=0):
    return spec((None, length, width), lambda b, h: (b, 0, first + h))


def per_head(*block):
    return spec((None, None) + block, lambda b, h: (b, h) + (0,) * len(block))


def gathered(devices, rows, width, at=0):
    return spec((devices, None, None, rows, width), lambda b, h: (0, b, h, 0, at))


def whole(*block):
    return spec((None,) + block, lambda b, h: (b,) + (0,) * len(block))


def call(body, name, seqs, args, in_specs, out_specs, outs, flops):
    size = sum(a.size * a.dtype.itemsize for a in args) + sum(
        o.size * o.dtype.itemsize for o in outs
    )
    return pl.pallas_call(
        body,
        grid=(seqs, H),
        in_specs=in_specs,
        out_specs=out_specs,
        out_shape=outs,
        name=name,
        cost_estimate=pl.CostEstimate(flops=flops, bytes_accessed=size, transcendentals=0),
    )(*args)


def conv_silu(padded, kernel):
    length = padded.shape[1] - (CONV - 1)
    total = kernel[0] * padded[:, 0:length]
    for offset in range(1, CONV):
        total = total + kernel[offset] * padded[:, offset : offset + length]
    return jax.nn.silu(total)


def rates(rate_in, decay_log, decay_bias):
    length = rate_in.shape[1]
    decays = -jnp.exp(decay_log) * jax.nn.softplus(rate_in[..., :H] + decay_bias)
    lower = jnp.tril(jnp.ones((length, length), F32))
    cumul = jnp.einsum("ts,bsh->bth", lower, decays, precision=exact_mode)
    return cumul, jax.nn.sigmoid(rate_in[..., H:])


def shifted(shard, axis, by):
    devices = lax.axis_size(axis)
    pairs = [(i, i + by) for i in range(devices) if 0 <= i + by < devices]
    return lax.ppermute(shard, axis, pairs)


def rms_back(inputs, scale, gain, upstream):
    normal = inputs * scale
    weighted = upstream * gain
    gain_grad = jnp.sum(upstream * normal, axis=0)
    return (scale * (weighted - normal * jnp.mean(weighted * normal, -1, keepdims=True)), gain_grad)


def gather(w):
    return lax.all_gather(w, ALL, axis=0, tiled=True)


def gather_all(parts):
    width = parts[0].shape[1]
    shares = gather(jnp.concatenate(parts, 0)).reshape(-1, sum(p.shape[0] for p in parts), width)
    found, start = [], 0
    for p in parts:
        found.append(shares[:, start : start + p.shape[0]].reshape(-1, width))
        start += p.shape[0]
    return found


def scatter_all(grads, devices):
    shares = [g.astype(BF16).reshape(devices, -1, g.shape[1]) for g in grads]
    sent = jnp.concatenate(shares, 1)
    own = lax.psum_scatter(
        sent.reshape(-1, sent.shape[2]), ALL, scatter_dimension=0, tiled=True
    ).astype(F32)
    found, start = [], 0
    for p in shares:
        found.append(own[start : start + p.shape[1]])
        start += p.shape[1]
    return found


def mm(a, b):
    return jnp.dot(a, b, preferred_element_type=F32)


def local(
    hidden_in, mixer_gain, mixer_proj, decay_proj, conv_kernel, decay_log, decay_bias,
    output_gain, mixer_out, ffn_gain, ffn_up, ffn_down, cotangent,
):
    seqs, length, feat = hidden_in.shape
    rows = seqs * length
    conv_width = 2 * QK + VV
    proj_cols = conv_width + VV
    rate_cols = 2 * H
    devices = lax.axis_size("ctx")
    place = jnp.reshape(lax.axis_index("ctx"), (1,)).astype(jnp.int32)
    sds = jax.ShapeDtypeStruct

    w_in = gather(
        jnp.concatenate(
            [mixer_proj, decay_proj, jnp.zeros((mixer_proj.shape[0], LANE - rate_cols), BF16)], 1
        )
    )
    w_out, up_1, up_2, down = gather_all((mixer_out, ffn_up[0], ffn_up[1], ffn_down))

    flat_in = hidden_in.reshape(rows, feat)
    scale_in = lax.rsqrt(jnp.mean(flat_in * flat_in, -1, keepdims=True) + norm_eps)
    normed = (flat_in * scale_in * mixer_gain).astype(BF16)
    cot_flat = cotangent.reshape(rows, feat)
    cot_rows = cot_flat.astype(BF16)

    projected = mm(normed, w_in).reshape(seqs, length, -1)
    pre_rows = projected[..., :conv_width]
    rate_in = projected[..., proj_cols : proj_cols + rate_cols]
    edge_rows = shifted(pre_rows[:, length - (CONV - 1) :], "ctx", 1)
    padded = jnp.concatenate([edge_rows, pre_rows], 1)
    act, conv_back = jax.vjp(conv_silu, padded, conv_kernel)
    (cumul, beta), rates_back = jax.vjp(rates, rate_in, decay_log, decay_bias)
    cumul_row = jnp.swapaxes(cumul, 1, 2)[:, :, None, :]

    qkv = [cols(length, DK), cols(length, DK, QK // DK), cols(length, DV, 2 * QK // DV)]
    narrow = [whole(length, H), per_head(1, length), whole(length, H)]
    work = seqs * H * length * length * DV
    local_out, query_map, own_state, inverse = call(
        core_fwd, "core_fwd", seqs,
        (act, act, act, cumul, cumul_row, beta),
        qkv + narrow,
        [cols(length, DV), cols(length, DK), per_head(DK, DV + DK), per_head(length, length)],
        [
            sds((seqs, length, VV), F32),
            sds((seqs, length, QK), F32),
            sds((seqs, H, DK, DV + DK), BF16),
            sds((seqs, H, length, length), F32),
        ],
        200 * work,
    )
    states = lax.all_gather(own_state, "ctx")
    gain_row = output_gain.reshape(1, DV)
    gain_spec = spec((1, DV), lambda b, h: (0, 0))
    place_spec = pl.BlockSpec(memory_space=pltpu.SMEM)
    gate_spec = cols(length, DV, conv_width // DV)
    gated, state_in = call(
        gate_fwd, "gate_fwd", seqs,
        (place, states, local_out, query_map, projected, gain_row),
        [place_spec, gathered(devices, DK, DV + DK), cols(length, DV), cols(length, DK),
         gate_spec, gain_spec],
        [cols(length, DV), per_head(DK, DV)],
        [sds((seqs, length, VV), BF16), sds((seqs, H, DK, DV), F32)],
        20 * work,
    )
    gated_rows = gated.reshape(rows, VV)
    residual = flat_in + mm(gated_rows, w_out)
    scale_mid = lax.rsqrt(jnp.mean(residual * residual, -1, keepdims=True) + norm_eps)
    ffn_rows = (residual * scale_mid * ffn_gain).astype(BF16)

    up_one, up_two = mm(ffn_rows, up_1.T), mm(ffn_rows, up_2.T)
    sigma = jax.nn.sigmoid(up_one)
    activ = (up_one * sigma * up_two).astype(BF16)
    block_out = residual + mm(activ, down)
    d_activ = mm(cot_rows, down.T)
    d_one = (d_activ * up_two * sigma * (1.0 + up_one * (1.0 - sigma))).astype(BF16)
    d_two = (d_activ * up_one * sigma).astype(BF16)
    down_grad = mm(activ.T, cot_rows).astype(BF16)
    up_grads = [mm(d_one.T, ffn_rows).astype(BF16), mm(d_two.T, ffn_rows).astype(BF16)]
    d_ffn = mm(d_one, up_1) + mm(d_two, up_2)

    d_res_part, gain_two_grad = rms_back(residual, scale_mid, ffn_gain, d_ffn)
    d_residual = cot_flat + d_res_part
    d_res_rows = d_residual.astype(BF16)
    out_grad = mm(gated_rows.T, d_res_rows).astype(BF16)
    d_gated = mm(d_res_rows, w_out.T).reshape(seqs, length, VV)
    d_mixed, d_gate, own_ds, gain_out_part = call(
        gate_bwd, "gate_bwd", seqs,
        (d_gated, local_out, query_map, state_in, projected, gain_row),
        [cols(length, DV), cols(length, DV), cols(length, DK), per_head(DK, DV), gate_spec,
         gain_spec],
        [cols(length, DV), cols(length, DV), per_head(DK, DV), per_head(1, DV)],
        [
            sds((seqs, length, VV), F32),
            sds((seqs, length, VV), BF16),
            sds((seqs, H, DK, DV), BF16),
            sds((seqs, H, 1, DV), F32),
        ],
        20 * work,
    )
    d_states = lax.all_gather(own_ds, "ctx")
    d_q, d_k, d_v, d_cols, d_rows = call(
        core_bwd, "core_bwd", seqs,
        (place, states, d_states, act, act, act, cumul, cumul_row, beta, inverse, state_in, d_mixed),
        [place_spec, gathered(devices, DK, DK, DV // DK), gathered(devices, DK, DV)]
        + qkv + narrow
        + [per_head(length, length), per_head(DK, DV), cols(length, DV)],
        [cols(length, DK), cols(length, DK), cols(length, DV), per_head(length, 2),
         per_head(1, length)],
        [
            sds((seqs, length, QK), F32),
            sds((seqs, length, QK), F32),
            sds((seqs, length, VV), F32),
            sds((seqs, H, length, 2), F32),
            sds((seqs, H, 1, length), F32),
        ],
        120 * work,
    )
    d_padded, kernel_grad = conv_back(jnp.concatenate([d_q, d_k, d_v], -1))
    d_cumul = jnp.swapaxes(d_cols[..., 0] + d_rows[:, :, 0], 1, 2)
    d_beta = jnp.swapaxes(d_cols[..., 1], 1, 2)
    d_rate, log_grad, bias_grad = rates_back((d_cumul, d_beta))
    d_edge = shifted(d_padded[:, : CONV - 1], "ctx", -1)
    d_pre = d_padded[:, CONV - 1 :].at[:, length - (CONV - 1) :].add(d_edge)
    d_proj = jnp.concatenate(
        [
            d_pre.reshape(rows, conv_width).astype(BF16),
            d_gate.reshape(rows, VV),
            d_rate.reshape(rows, rate_cols).astype(BF16),
            jnp.zeros((rows, LANE - rate_cols), BF16),
        ],
        1,
    )
    in_grad = mm(normed.T, d_proj)
    parts = [in_grad[:, at : at + feat] for at in range(0, proj_cols, feat)]
    rate_grad = in_grad[:, proj_cols : proj_cols + rate_cols]
    down_shard, up_s1, up_s2, out_shard, *in_shards = scatter_all(
        [down_grad] + up_grads + [out_grad] + parts, devices * lax.axis_size("shard")
    )
    up_shard = jnp.stack([up_s1, up_s2])
    d_normed = mm(d_proj, w_in.T)
    d_in_part, gain_one_grad = rms_back(flat_in, scale_in, mixer_gain, d_normed)
    input_grad = d_residual + d_in_part

    small = (
        gain_one_grad, gain_two_grad, kernel_grad, log_grad, bias_grad,
        jnp.sum(gain_out_part, (0, 1, 2)), rate_grad,
    )
    flat = jnp.concatenate([s.reshape(-1) for s in small])
    pad = -flat.shape[0] % (8 * LANE)
    total = lax.psum(jnp.pad(flat, (0, pad)).reshape(-1, LANE), ALL).reshape(-1)
    sums, start = [], 0
    for s in small:
        sums.append(total[start : start + s.size].reshape(s.shape))
        start += s.size
    own_rows = decay_proj.shape[0]
    me = lax.axis_index("shard") * devices + lax.axis_index("ctx")
    rate_shard = lax.dynamic_slice_in_dim(sums[6], me * own_rows, own_rows, 0)
    return (
        block_out.reshape(seqs, length, feat),
        input_grad.reshape(seqs, length, feat),
        sums[0],
        jnp.concatenate(in_shards, 1),
        rate_shard,
        sums[2],
        sums[3],
        sums[4],
        sums[5],
        out_shard,
        sums[1],
        up_shard,
        down_shard,
    )


def solution(mesh):
    split = P(ALL, None)
    block = P("shard", "ctx", None)
    up = P(None, ALL, None)
    return jax.shard_map(
        local,
        mesh=mesh,
        in_specs=(block, P(), split, split, P(), P(), P(), P(), split, P(), up, split, block),
        out_specs=(block, block, P(), split, split, P(), P(), P(), P(), split, P(), up, split),
        check_vma=False,
    )
```
